32 devices in a mesh: seg: 8 (over y, x, core), col: 4 (over z).
Axes of the slice: x: 2, y: 2, z: 4, core: 2. Of those that a mesh axis runs over, the one named last changes fastest.
Arguments:
- design: bfloat16 [4096, 4096], P('seg', 'col'), may hold values from -6 to 6
- taps: bfloat16 [128], replicated, may hold values from -0.5 to 0.5
- seg_ids: int32 [4096], P('seg'), may hold values from 0 to 31, never falling along the last dimension, each value on 1 to 512 neighbouring positions
- block_home: int32 [4], replicated, may hold values from 0 to 3, each once
- block_row: int32 [1], replicated, may hold values from 0 to 3
Outputs:
- normal_rows: float32 [1024, 4096], P('seg', 'col')
The draws below stay inside these ranges and needn't reach their ends.
Inputs may be any that keep to these rules, and one draw needn't show every extreme that they name: seg_ids never falls along the observations; each data segment holds at most 512 observations. block_home holds each block position once.
All inputs are finite; a program needn't handle non-finite values.
Results may differ from the reference program's by a relative error of at most 0.0024.
Values may be sent and summed in bfloat16 or wider, within the bound.
No kernel may reach another device: no remote copies, remote signals or barrier semaphores. Data moves between devices by JAX's collectives and lax.ppermute only.
A program may use at most 64 MiB of HBM per device.

```python
import math
import jax
import jax.numpy as jnp
import numpy as np
from jax import lax

PANEL = 1024
TAPS = 128
OBS_DEV = 512
OBS = 4096
NCOL = 4096
NBLK = 4
N_SEG = 8


def block_levels(key, shape, shards, low, top_value):
    def one(dim, blocks):
        draws = jax.random.uniform(jax.random.fold_in(jax.random.fold_in(key, 6), dim), (blocks,), jnp.float32, low / len(shards), top_value / len(shards))
        return jnp.repeat(jnp.exp(draws), shape[dim] // blocks).reshape((-1,) + (1,) * (len(shape) - dim - 1))

    gain = one(*shards[0])
    for cut in shards[1:]:
        gain = gain * one(*cut)
    return gain


def split_up(number_of, total, bound, slope):
    loads = [(1 << 20) // math.isqrt(rank ** slope) + 1 for rank in range(2, number_of + 1)]
    rest, holding = total - bound - (number_of - 1), [1] * (number_of - 1)
    while rest > 0:
        candidates = [i for i in range(number_of - 1) if holding[i] < bound]
        pool, remaining = sum([loads[i] for i in candidates]), rest
        for i in candidates:
            more = min(bound - holding[i], max(1, remaining * loads[i] // pool), rest)
            holding[i] = holding[i] + more
            rest = rest - more
    return np.array([bound] + holding)


def ragged(own_key, amount, total, bound, slope):
    if amount == 2:
        one = jax.random.randint(own_key, (), max(1, total - bound), min(bound, total - 1) + 1)
        return jnp.stack([one, total - one])
    tallies = jnp.asarray(split_up(amount, total, bound, slope), jnp.int32)
    pairs = (amount - 1) // 2
    giver, receiver = tallies[1:1 + 2 * pairs:2], tallies[2:2 + 2 * pairs:2]
    margin = jnp.minimum(giver - 1, bound - receiver)
    shifted = jax.random.randint(jax.random.fold_in(own_key, 1), (pairs,), 0, 1 << 20) % (margin + 1)
    tallies = tallies.at[1:1 + 2 * pairs:2].set(giver - shifted).at[2:2 + 2 * pairs:2].set(receiver + shifted)
    return tallies[jax.random.permutation(jax.random.fold_in(own_key, 2), amount)]


def scatter_about(rng, extent, spread, most, shards=(), kind=jnp.bfloat16):
    array = jax.random.normal(rng, extent, jnp.float32) * spread
    if len(shards) > 0:
        array = block_levels(rng, extent, shards, -0.22, 0.18) * array
    return jnp.clip(array, min=-most, max=most).astype(kind)


def setup_inputs(seed: int = 0) -> dict:
    key_list = jax.random.split(jax.random.key(seed), 6)
    return {
        "design": scatter_about(key_list[0], (OBS, NCOL), 1.0, 6.0, ((0, 8), (1, 4))),
        "taps": scatter_about(key_list[1], (TAPS,), TAPS ** -0.5, 0.5),
        "seg_ids": jnp.searchsorted(jnp.cumsum(ragged(key_list[2], 4 * N_SEG, OBS, OBS_DEV, 0)), jnp.arange(OBS), side="right").astype(jnp.int32),
        "block_home": jax.random.permutation(key_list[3], NBLK).astype(jnp.int32),
        "block_row": jax.random.randint(key_list[4], (1,), 0, NBLK).astype(jnp.int32),
    }


def filter_blocks(taps, seg_ids):
    nblocks = OBS // TAPS
    sid_blocks = seg_ids.reshape(nblocks, TAPS)
    before = jnp.concatenate([jnp.zeros((1, TAPS), jnp.int32), sid_blocks[:-1]], axis=0)
    joined = jnp.concatenate([before, sid_blocks], axis=1)
    rows = jnp.arange(TAPS, dtype=jnp.int32)[:, None]
    cols = jnp.arange(2 * TAPS, dtype=jnp.int32)[None, :]
    lag = rows + TAPS - cols
    valid = (lag >= 0) & (lag < TAPS)
    toeplitz = jnp.where(valid, taps[jnp.clip(lag, 0, TAPS - 1)], jnp.zeros((), taps.dtype))
    same = sid_blocks[:, :, None] == joined[:, None, :]
    return jnp.where(same, toeplitz[None], jnp.zeros((), taps.dtype))

def apply_filter(columns, blocks):
    nblocks = OBS // TAPS
    width = columns.shape[1]
    current = columns.reshape(nblocks, TAPS, width).astype(jnp.float32)
    before = jnp.concatenate([jnp.zeros((1, TAPS, width), jnp.float32), current[:-1]], axis=0)
    mats = blocks.astype(jnp.float32)
    out = jnp.einsum('bij,bjc->bic', mats[:, :, :TAPS], before) + jnp.einsum('bij,bjc->bic', mats[:, :, TAPS:], current)
    return out.reshape(OBS, width).astype(jnp.bfloat16)

def reference(design, taps, seg_ids, block_home, block_row):
    blocks = filter_blocks(taps, seg_ids)
    place = block_home[block_row[0]].astype(jnp.int32)
    panel = apply_filter(lax.dynamic_slice_in_dim(design, place * PANEL, PANEL, 1), blocks)

    def one_block(index):
        cols = lax.dynamic_slice_in_dim(design, index * PANEL, PANEL, 1)
        filtered = apply_filter(cols, blocks)
        return lax.dot_general(panel, filtered, (((0,), (0,)), ((), ())), preferred_element_type=jnp.float32)
    tiles = lax.map(one_block, jnp.arange(NBLK, dtype=jnp.int32))
    normal = jnp.transpose(tiles, (1, 0, 2)).reshape(PANEL, NCOL)
    return normal * (1.0 / math.sqrt(OBS))
```

```python
import math

import jax
import jax.numpy as jnp
from jax import lax
from jax.experimental import pallas as pl
from jax.experimental.pallas import tpu as pltpu
from jax.sharding import PartitionSpec as P

PANEL = 1024
F32 = jnp.float32
BF16 = jnp.bfloat16
CONTRACT_ROWS = (((0,), (0,)), ((), ()))


def toeplitz(taps_row, width):
    lag = lax.broadcasted_iota(jnp.int32, (width, 2 * width), 0)
    col = lax.broadcasted_iota(jnp.int32, (width, 2 * width), 1)
    flip = (lag + col == width).astype(F32).astype(BF16)
    first = jnp.dot(jnp.broadcast_to(taps_row, (16, width)), flip, preferred_element_type=F32)
    tall = jnp.broadcast_to(first[:1], (width, 2 * width))
    return pltpu.roll(tall, 0, 1, stride=1, stride_axis=0)


def filter_rows(taps_row, sid, rim_sid, read):
    nblocks, width = sid.shape
    base = toeplitz(taps_row, width)
    for b in range(nblocks):
        before = rim_sid if b == 0 else sid[b - 1 : b]
        joined = jnp.concatenate([before, sid[b : b + 1]], axis=1)
        own = jnp.broadcast_to(sid[b : b + 1], (width, width)).T
        same = jnp.concatenate([own, own], axis=1) == jnp.broadcast_to(joined, (width, 2 * width))
        matrix = jnp.where(same, base, 0.0).astype(BF16)
        yield b, jnp.dot(matrix, read(b), preferred_element_type=F32).astype(BF16)


def filter_kernel(where_ref, taps_ref, sid_ref, rim_ref, design_ref, out_ref, *pieces):
    width = sid_ref.shape[1]
    rim_sid = rim_ref[width : width + 16, :width].astype(F32)[:1].astype(jnp.int32)

    def read(b):
        if b == 0:
            return jnp.concatenate([rim_ref[:width], design_ref[:width]], axis=0)
        return design_ref[(b - 1) * width : (b + 1) * width]

    for b, rows in filter_rows(taps_ref[...], sid_ref[...], rim_sid, read):
        out_ref[b * width : (b + 1) * width] = rows
    for k, piece in enumerate(pieces):
        half = piece.shape[1] // 2
        for side in range(2):
            start = pl.multiple_of(where_ref[k] * 2 * half + where_ref[len(pieces) + side] * half, 128)
            piece[:, side * half : (side + 1) * half] = out_ref[:, pl.ds(start, half)]


def filtered(where, taps, sid, rim, design, npieces, cut):
    rows, cols = design.shape
    width = taps.shape[0]
    shapes = [jax.ShapeDtypeStruct((rows, cols), BF16)]
    shapes += [jax.ShapeDtypeStruct((rows, cut), BF16)] * npieces
    vmem = pl.BlockSpec(memory_space=pltpu.VMEM)
    return pl.pallas_call(
        filter_kernel,
        in_specs=[pl.BlockSpec(memory_space=pltpu.SMEM)] + [vmem] * 4,
        out_specs=[vmem] * len(shapes),
        out_shape=shapes,
        compiler_params=pltpu.CompilerParams(vmem_limit_bytes=32 << 20),
    )(where, taps.reshape(1, width), sid.reshape(-1, width), rim, design)


def with_sids(design, sid, width):
    row = jnp.zeros((16, design.shape[1]), BF16).at[0, :width].set(sid[-width:].astype(BF16))
    return jnp.concatenate([design[-width:], row], axis=0)


def tile(panel, rows):
    return lax.dot_general(panel, rows, CONTRACT_ROWS, preferred_element_type=F32)


def relayed(pieces, place, owner):
    if owner in (1, 2):
        middle = 3 - owner
        ends = [(middle, 3 * (middle - 1)), (owner, 3 * (owner - 1))]
    else:
        middle = 2 if owner == 0 else 1
        ends = None
    for piece in pieces:
        got = lax.ppermute(piece, "col", [(owner, middle)])
        if ends:
            held = jnp.where(place == owner, piece, got)
            far = lax.ppermute(held, "col", ends)
            yield jnp.where((place == owner) | (place == middle), held, far)
        else:
            low = lax.ppermute(got, "col", [(middle, middle - 1)])
            high = lax.ppermute(got, "col", [(middle, middle + 1)])
            yield jnp.where(
                place == owner,
                piece,
                jnp.where(place == middle, got, jnp.where(place == middle - 1, low, high)),
            )


def sliced_panel(scale):
    def run(owner, design, taps, sid):
        width = taps.shape[0]
        nseg = lax.axis_size("seg")
        seg, place = lax.axis_index("seg"), lax.axis_index("col")
        chip, core = seg // 2, seg % 2
        order = (3, 1, 2, 0)
        where = jnp.stack([chip ^ k for k in order] + [1 - core, core]).astype(jnp.int32)
        rim = lax.ppermute(with_sids(design, sid, width), "seg", [(s, s + 1) for s in range(nseg - 1)])
        cut = PANEL // len(order)
        rows, *pieces = filtered(where, taps, sid, rim, design, len(order), cut)
        total = []
        for k, panel in zip(order, relayed(pieces, place, owner)):
            theirs = tile(panel[:, : cut // 2], rows)
            mine = tile(panel[:, cut // 2 :], rows)
            mine = mine + lax.ppermute(theirs, "seg", [(s, s ^ 1) for s in range(nseg)])
            if k:
                sent = lax.ppermute(mine.astype(BF16), "seg", [(s, s ^ (2 * k)) for s in range(nseg)])
                mine = sent.astype(F32)
            total.append(mine)
        return (total[3] + total[0] + total[1] + total[2]) * scale

    return run


def spread(value, axis, source):
    kept = jnp.where(lax.axis_index(axis) == source, value, 0).astype(value.dtype)
    return lax.psum(kept, axis)


def any_mesh(scale):
    def run(owner, design, taps, sid):
        width = taps.shape[0]
        nseg = lax.axis_size("seg")
        rim = lax.ppermute(with_sids(design, sid, width), "seg", [(s, s + 1) for s in range(nseg - 1)])
        rows = filtered(jnp.zeros((8,), jnp.int32), taps, sid, rim, design, 0, 0)[0]
        panel = spread(rows, "col", owner)
        summed = lax.psum_scatter(tile(panel, rows), "seg", scatter_dimension=0, tiled=True)
        return summed * scale

    return run


def solution(mesh):
    nseg, ncol = mesh.shape["seg"], mesh.shape["col"]

    def shards(design, taps, seg_ids, block_home, block_row):
        scale = 1.0 / math.sqrt(design.shape[0] * nseg)
        owner = block_home[block_row[0]] // (design.shape[1] // PANEL)
        if (nseg, ncol, design.shape[1]) == (8, 4, PANEL):
            run = sliced_panel(scale)
            branches = [lambda *a, o=o: run(o, *a) for o in range(ncol)]
            return lax.switch(owner, branches, design, taps, seg_ids)
        return any_mesh(scale)(owner, design, taps, seg_ids)

    placed = (P("seg", "col"), P(), P("seg"), P(), P())
    return jax.shard_map(
        shards, mesh=mesh, in_specs=placed, out_specs=P("seg", "col"), check_vma=False
    )
```

```python
import functools
import math

import jax
import jax.numpy as jnp
from jax import lax
from jax.experimental import pallas as pl
from jax.experimental.pallas import tpu as pltpu
from jax.sharding import PartitionSpec as P

PANEL = 1024
F32 = jnp.float32
BF16 = jnp.bfloat16
CONTRACT_ROWS = (((0,), (0,)), ((), ()))


def toeplitz(taps_row, width):
    lag = lax.broadcasted_iota(jnp.int32, (width, 2 * width), 0)
    col = lax.broadcasted_iota(jnp.int32, (width, 2 * width), 1)
    flip = (lag + col == width).astype(F32).astype(BF16)
    first = jnp.dot(jnp.broadcast_to(taps_row, (16, width)), flip, preferred_element_type=F32)
    tall = jnp.broadcast_to(first[:1], (width, 2 * width))
    return pltpu.roll(tall, 0, 1, stride=1, stride_axis=0)


def segment_matrix(base, own, joined):
    width = base.shape[0]
    tall = jnp.broadcast_to(own, (width, width)).T
    same = jnp.concatenate([tall, tall], axis=1) == jnp.broadcast_to(joined, (width, 2 * width))
    return jnp.where(same, base, 0.0).astype(BF16)


def cut_pieces(where_ref, rows_ref, pieces, plan):
    for piece, parts in zip(pieces, plan, strict=True):
        at, lanes = 0, piece.shape[1]
        for lo, hi, group in parts:
            start = ((where_ref[0] ^ ORDER[group]) * 2 + where_ref[1]) * lanes
            cols = pl.ds(pl.multiple_of(start, 128), lanes)
            piece[at : at + hi - lo] = rows_ref[lo:hi, cols]
            at += hi - lo


def edge_kernel(sid_ref, design_ref, edge_ref, sem):
    width = sid_ref.shape[1]
    rows = design_ref.shape[0]
    copy = pltpu.make_async_copy(design_ref.at[rows - width : rows], edge_ref.at[:width], sem)
    copy.start()
    edge_ref[width:] = jnp.zeros((16, edge_ref.shape[1]), BF16)
    last = sid_ref[sid_ref.shape[0] - 1 :]
    edge_ref[width:, :width] = jnp.broadcast_to(last, (16, width)).astype(F32).astype(BF16)
    copy.wait()


def edge_kernel(sid_ref, design_ref, edge_ref, sem):
    width = sid_ref.shape[1]
    rows = design_ref.shape[0]
    copy = pltpu.make_async_copy(design_ref.at[rows - width : rows], edge_ref.at[:width], sem)
    copy.start()
    edge_ref[width:] = jnp.zeros((16, edge_ref.shape[1]), BF16)
    last = sid_ref[sid_ref.shape[0] - 1 :]
    edge_ref[width:, :width] = jnp.broadcast_to(last, (16, width)).astype(F32).astype(BF16)
    copy.wait()


def cut_kernel(plan, where_ref, rows_ref, *pieces):
    cut_pieces(where_ref, rows_ref, pieces, plan)


def inner_kernel(where_ref, home_ref, row_ref, taps_ref, sid_ref, design_ref, out_ref, base_ref, owner_ref):
    nblocks, width = sid_ref.shape
    owner_ref[0] = home_ref[row_ref[0]]
    base = toeplitz(taps_ref[...], width)
    base_ref[...] = base.astype(BF16)
    sid = sid_ref[...]
    for b in range(1, nblocks):
        joined = jnp.concatenate([sid[b - 1 : b], sid[b : b + 1]], axis=1)
        matrix = segment_matrix(base, sid[b : b + 1], joined)
        rows = design_ref[(b - 1) * width : (b + 1) * width]
        out_ref[(b - 1) * width : b * width] = jnp.dot(
            matrix, rows, preferred_element_type=F32
        ).astype(BF16)


def rim_kernel(plan, where_ref, base_ref, sid_ref, design_ref, rim_ref, inner_ref, out_ref, *pieces):
    width = sid_ref.shape[1]
    sid = sid_ref[:1]
    rim_sid = rim_ref[width : width + 16, :width].astype(F32)[:1].astype(jnp.int32)
    rim_sid = jnp.where(where_ref[0] + where_ref[1] == 0, -1, rim_sid)
    joined = jnp.concatenate([rim_sid, sid], axis=1)
    matrix = segment_matrix(base_ref[...].astype(F32), sid, joined)
    rows = jnp.concatenate([rim_ref[:width], design_ref[:width]], axis=0)
    out_ref[:width] = jnp.dot(matrix, rows, preferred_element_type=F32).astype(BF16)
    out_ref[width:] = inner_ref[...]
    cut_pieces(where_ref, out_ref, pieces, plan)


VMEM = pl.BlockSpec(memory_space=pltpu.VMEM)
SMEM = pl.BlockSpec(memory_space=pltpu.SMEM)


def piece_shape(rows, plan):
    return [jax.ShapeDtypeStruct((sum(hi - lo for lo, hi, _ in parts), LANES), BF16) for parts in plan]


def last_rows(sid, design, width):
    cols = design.shape[1]
    return pl.pallas_call(
        edge_kernel,
        in_specs=[VMEM, pl.BlockSpec(memory_space=pl.ANY)],
        out_specs=VMEM,
        scratch_shapes=[pltpu.SemaphoreType.DMA],
        out_shape=jax.ShapeDtypeStruct((width + 16, cols), BF16),
        compiler_params=pltpu.CompilerParams(vmem_limit_bytes=8 << 20),
    )(sid.reshape(-1, width), design)


def filter_inner(where, home, row, taps, sid, design):
    rows, cols = design.shape
    width = taps.shape[0]
    shapes = [
        jax.ShapeDtypeStruct((rows - width, cols), BF16),
        jax.ShapeDtypeStruct((width, 2 * width), BF16),
        jax.ShapeDtypeStruct((1,), jnp.int32),
    ]
    return pl.pallas_call(
        inner_kernel,
        in_specs=[SMEM] * 3 + [VMEM] * 3,
        out_specs=[VMEM] * 2 + [SMEM],
        out_shape=shapes,
        compiler_params=pltpu.CompilerParams(vmem_limit_bytes=8 << 20),
    )(where, home, row, taps.reshape(1, width), sid.reshape(-1, width), design)


def filter_rim(where, base, sid, design, rim, inner, plan):
    rows, cols = design.shape
    width = base.shape[0]
    shapes = [jax.ShapeDtypeStruct((rows, cols), BF16)] + piece_shape(rows, plan)
    return pl.pallas_call(
        functools.partial(rim_kernel, plan),
        in_specs=[SMEM] + [VMEM] * 5,
        out_specs=[VMEM] * len(shapes),
        out_shape=shapes,
        compiler_params=pltpu.CompilerParams(vmem_limit_bytes=8 << 20),
    )(where, base, sid.reshape(-1, width), design, rim, inner)


def tile(panel, rows):
    return lax.dot_general(panel, rows, CONTRACT_ROWS, preferred_element_type=F32)


def from_before(value):
    nseg = lax.axis_size("seg")
    with jax.named_scope("rim"):
        return lax.ppermute(value, "seg", [(s, (s + 1) % nseg) for s in range(nseg)])


def exchanged(value, bits, name):
    nseg = lax.axis_size("seg")
    with jax.named_scope(f"swap_{name}"):
        return lax.ppermute(value, "seg", [(s, s ^ bits) for s in range(nseg)])


ORDER = (3, 1, 2, 0)
LANES = 128
OUTER = ((3, "s", 0), (3, "s", 1))
INNER = ((3, "s", 0), (3, "s", 1))
OUTER_LANDED = (0, 1)
INNER_LANDED = ()


def hop(value, pairs, name):
    with jax.named_scope(f"step_{name}"):
        return lax.ppermute(value, "col", pairs)


def sliced_panel(owner, where, rows, *own):
    place = lax.axis_index("col")
    middle = (2, 2, 1, 1)[owner]
    half = rows.shape[0]
    theirs = exchanged(rows, 1, "pair")
    cols = [((where[0] ^ k) * 2 + where[1]) * LANES for k in ORDER]
    other = [lax.dynamic_slice_in_dim(theirs, c, LANES, axis=1) for c in cols]
    pieces = [jnp.concatenate([o, p], axis=0) for o, p in zip(own, other)]
    pieces = list(lax.optimization_barrier(tuple(pieces)))
    got = [hop(piece, [(owner, middle)], f"a{n}") for n, piece in enumerate(pieces)]
    sums, landed, far = [None] * 4, [None] * 4, []

    def summed(group, own, paired):
        total = tile(own, rows) + tile(paired, theirs)
        if ORDER[group]:
            sums[group] = total.astype(BF16)
            landed[group] = exchanged(sums[group], 2 * ORDER[group], f"g{group}")
        return total

    for n, piece in enumerate(pieces):
        held = jnp.where(place == owner, piece, got[n]) if owner in (1, 2) else got[n]
        for at, kind, group in INNER if owner in (1, 2) else OUTER:
            if at == n:
                made = {"s": sums, "l": landed}[kind]
                held, made[group] = lax.optimization_barrier((held, made[group]))
        if owner in (1, 2):
            ends = [(middle, 3 * (middle - 1)), (owner, 3 * (owner - 1))]
            out = hop(held, ends, f"b{n}")
            far.append(jnp.where((place == owner) | (place == middle), held, out))
        else:
            low = hop(held, [(middle, middle - 1)], f"b{n}")
            high = hop(held, [(middle, middle + 1)], f"c{n}")
            out = jnp.where(place == middle - 1, low, high)
            far.append(jnp.where(place == owner, piece, jnp.where(place == middle, held, out)))
        panel = far[n]
        if n == 3:
            for g in INNER_LANDED if owner in (1, 2) else OUTER_LANDED:
                landed[g], panel = lax.optimization_barrier((landed[g], panel))
        total = summed(n, panel[:half], panel[half:])
    for part in landed[:3]:
        total = total + part.astype(F32)
    return total


def spread(value, axis, source):
    kept = jnp.where(lax.axis_index(axis) == source, value, 0).astype(value.dtype)
    return lax.psum(kept, axis)


def any_mesh(owner, where, rows):
    panel = spread(rows, "col", owner)
    return lax.psum_scatter(tile(panel, rows), "seg", scatter_dimension=0, tiled=True)


def solution(mesh):
    nseg, ncol = mesh.shape["seg"], mesh.shape["col"]

    def shards(design, taps, seg_ids, block_home, block_row):
        sliced = (nseg, ncol, design.shape[1]) == (8, 4, PANEL)
        scale = 1.0 / math.sqrt(design.shape[0] * nseg)
        seg = lax.axis_index("seg")
        where = jnp.stack([lax.shift_right_logical(seg, 1), seg & 1]).astype(jnp.int32)
        rim = from_before(last_rows(seg_ids, design, taps.shape[0]))
        inner, base, home = filter_inner(where, block_home, block_row, taps, seg_ids, design)
        owner = home[0] // (design.shape[1] // PANEL)
        count = design.shape[0]
        plan = [((0, count, n),) for n in range(len(ORDER))]
        made = filter_rim(where, base, seg_ids, design, rim, inner, plan if sliced else [])
        if sliced:
            branches = [lambda *a, o=o: sliced_panel(o, *a) * scale for o in range(ncol)]
            return lax.switch(owner, branches, where, *made)
        return any_mesh(owner, where, *made) * scale

    placed = (P("seg", "col"), P(), P("seg"), P(), P())
    return jax.shard_map(
        shards, mesh=mesh, in_specs=placed, out_specs=P("seg", "col"), check_vma=False
    )
```

```python
import functools
import math

import jax
import jax.numpy as jnp
from jax import lax
from jax.experimental import pallas as pl
from jax.experimental.pallas import tpu as pltpu
from jax.sharding import PartitionSpec as P

PANEL = 1024
F32 = jnp.float32
BF16 = jnp.bfloat16
CONTRACT_ROWS = (((0,), (0,)), ((), ()))


def toeplitz(taps_row, width):
    lag = lax.broadcasted_iota(jnp.int32, (width, 2 * width), 0)
    col = lax.broadcasted_iota(jnp.int32, (width, 2 * width), 1)
    flip = (lag + col == width).astype(F32).astype(BF16)
    first = jnp.dot(jnp.broadcast_to(taps_row, (16, width)), flip, preferred_element_type=F32)
    tall = jnp.broadcast_to(first[:1], (width, 2 * width))
    return pltpu.roll(tall, 0, 1, stride=1, stride_axis=0)


def segment_matrix(base, own, joined):
    width = base.shape[0]
    tall = jnp.broadcast_to(own, (width, width)).T
    same = jnp.concatenate([tall, tall], axis=1) == jnp.broadcast_to(joined, (width, 2 * width))
    return jnp.where(same, base, 0.0).astype(BF16)


def cut_pieces(where_ref, rows_ref, pieces, plan):
    for piece, parts in zip(pieces, plan, strict=True):
        at, lanes = 0, piece.shape[1]
        for lo, hi, group in parts:
            start = ((where_ref[0] ^ ORDER[group]) * 2 + where_ref[1]) * lanes
            cols = pl.ds(pl.multiple_of(start, 128), lanes)
            piece[at : at + hi - lo] = rows_ref[lo:hi, cols]
            at += hi - lo


def inner_kernel(where_ref, home_ref, row_ref, taps_ref, sid_ref, design_ref, out_ref, base_ref, owner_ref):
    nblocks, width = sid_ref.shape
    owner_ref[0] = home_ref[row_ref[0]]
    base = toeplitz(taps_ref[...], width)
    base_ref[...] = base.astype(BF16)
    sid = sid_ref[...]
    for b in range(1, nblocks):
        joined = jnp.concatenate([sid[b - 1 : b], sid[b : b + 1]], axis=1)
        matrix = segment_matrix(base, sid[b : b + 1], joined)
        rows = design_ref[(b - 1) * width : (b + 1) * width]
        out_ref[(b - 1) * width : b * width] = jnp.dot(
            matrix, rows, preferred_element_type=F32
        ).astype(BF16)


def rim_kernel(plan, where_ref, base_ref, sid_ref, design_ref, rim_ref, inner_ref, out_ref, *pieces):
    width = sid_ref.shape[1]
    sid = sid_ref[:1]
    rim_sid = rim_ref[width : width + 16, :width].astype(F32)[:1].astype(jnp.int32)
    rim_sid = jnp.where(where_ref[0] + where_ref[1] == 0, -1, rim_sid)
    joined = jnp.concatenate([rim_sid, sid], axis=1)
    matrix = segment_matrix(base_ref[...].astype(F32), sid, joined)
    rows = jnp.concatenate([rim_ref[:width], design_ref[:width]], axis=0)
    out_ref[:width] = jnp.dot(matrix, rows, preferred_element_type=F32).astype(BF16)
    out_ref[width:] = inner_ref[...]
    cut_pieces(where_ref, out_ref, pieces, plan)


VMEM = pl.BlockSpec(memory_space=pltpu.VMEM)
SMEM = pl.BlockSpec(memory_space=pltpu.SMEM)


def piece_shape(rows, plan):
    return [jax.ShapeDtypeStruct((sum(hi - lo for lo, hi, _ in parts), LANES), BF16) for parts in plan]


def last_rows(sid, design, width):
    row = jnp.zeros((16, design.shape[1]), BF16).at[0, :width].set(sid[-width:].astype(BF16))
    return jnp.concatenate([design[-width:], row], axis=0)


def filter_inner(where, home, row, taps, sid, design):
    rows, cols = design.shape
    width = taps.shape[0]
    shapes = [
        jax.ShapeDtypeStruct((rows - width, cols), BF16),
        jax.ShapeDtypeStruct((width, 2 * width), BF16),
        jax.ShapeDtypeStruct((1,), jnp.int32),
    ]
    return pl.pallas_call(
        inner_kernel,
        in_specs=[SMEM] * 3 + [VMEM] * 3,
        out_specs=[VMEM] * 2 + [SMEM],
        out_shape=shapes,
        compiler_params=pltpu.CompilerParams(vmem_limit_bytes=8 << 20),
    )(where, home, row, taps.reshape(1, width), sid.reshape(-1, width), design)


def filter_rim(where, base, sid, design, rim, inner, plan):
    rows, cols = design.shape
    width = base.shape[0]
    shapes = [jax.ShapeDtypeStruct((rows, cols), BF16)] + piece_shape(rows, plan)
    return pl.pallas_call(
        functools.partial(rim_kernel, plan),
        in_specs=[SMEM] + [VMEM] * 5,
        out_specs=[VMEM] * len(shapes),
        out_shape=shapes,
        compiler_params=pltpu.CompilerParams(vmem_limit_bytes=8 << 20),
    )(where, base, sid.reshape(-1, width), design, rim, inner)


def tile(panel, rows):
    return lax.dot_general(panel, rows, CONTRACT_ROWS, preferred_element_type=F32)


def from_before(value):
    nseg = lax.axis_size("seg")
    with jax.named_scope("rim"):
        return lax.ppermute(value, "seg", [(s, (s + 1) % nseg) for s in range(nseg)])


def exchanged(value, bits, name):
    nseg = lax.axis_size("seg")
    with jax.named_scope(f"swap_{name}"):
        return lax.ppermute(value, "seg", [(s, s ^ bits) for s in range(nseg)])


ORDER = (3, 1, 2, 0)
LANES = 128
OUTER = ((2, 0), (3, 1))
INNER = ((3, 1),)


def hop(value, pairs, name):
    with jax.named_scope(f"step_{name}"):
        return lax.ppermute(value, "col", pairs)


def sliced_panel(owner, where, rows, *own):
    place = lax.axis_index("col")
    middle = (2, 2, 1, 1)[owner]
    half = rows.shape[0]
    theirs = exchanged(rows, 1, "pair")
    cols = [((where[0] ^ k) * 2 + where[1]) * LANES for k in ORDER]
    other = [lax.dynamic_slice_in_dim(theirs, c, LANES, axis=1) for c in cols]
    pieces = [jnp.concatenate([o, p], axis=0) for o, p in zip(own, other)]
    got = [hop(piece, [(owner, middle)], f"a{n}") for n, piece in enumerate(pieces)]
    sums, landed, far = [None] * 4, [None] * 4, []

    def summed(group, own, paired):
        total = tile(own, rows) + tile(paired, theirs)
        if ORDER[group]:
            sums[group] = total.astype(BF16)
            landed[group] = exchanged(sums[group], 2 * ORDER[group], f"g{group}")
        return total

    for n, piece in enumerate(pieces):
        held = jnp.where(place == owner, piece, got[n]) if owner in (1, 2) else got[n]
        for at, group in INNER if owner in (1, 2) else OUTER:
            if at == n:
                held, sums[group] = lax.optimization_barrier((held, sums[group]))
        if owner in (1, 2):
            ends = [(middle, 3 * (middle - 1)), (owner, 3 * (owner - 1))]
            out = hop(held, ends, f"b{n}")
            far.append(jnp.where((place == owner) | (place == middle), held, out))
        else:
            low = hop(held, [(middle, middle - 1)], f"b{n}")
            high = hop(held, [(middle, middle + 1)], f"c{n}")
            out = jnp.where(place == middle - 1, low, high)
            far.append(jnp.where(place == owner, piece, jnp.where(place == middle, held, out)))
        panel = far[n]
        total = summed(n, panel[:half], panel[half:])
    for part in landed[:3]:
        total = total + part.astype(F32)
    return total


def spread(value, axis, source):
    kept = jnp.where(lax.axis_index(axis) == source, value, 0).astype(value.dtype)
    return lax.psum(kept, axis)


def any_mesh(owner, where, rows):
    panel = spread(rows, "col", owner)
    return lax.psum_scatter(tile(panel, rows), "seg", scatter_dimension=0, tiled=True)


def solution(mesh):
    nseg, ncol = mesh.shape["seg"], mesh.shape["col"]

    def shards(design, taps, seg_ids, block_home, block_row):
        sliced = (nseg, ncol, design.shape[1]) == (8, 4, PANEL)
        scale = 1.0 / math.sqrt(design.shape[0] * nseg)
        seg = lax.axis_index("seg")
        where = jnp.stack([lax.shift_right_logical(seg, 1), seg & 1]).astype(jnp.int32)
        rim = from_before(last_rows(seg_ids, design, taps.shape[0]))
        inner, base, home = filter_inner(where, block_home, block_row, taps, seg_ids, design)
        owner = home[0] // (design.shape[1] // PANEL)
        count = design.shape[0]
        plan = [((0, count, n),) for n in range(len(ORDER))]
        made = filter_rim(where, base, seg_ids, design, rim, inner, plan if sliced else [])
        if sliced:
            branches = [lambda *a, o=o: sliced_panel(o, *a) * scale for o in range(ncol)]
            return lax.switch(owner, branches, where, *made)
        return any_mesh(owner, where, *made) * scale

    placed = (P("seg", "col"), P(), P("seg"), P(), P())
    return jax.shard_map(
        shards, mesh=mesh, in_specs=placed, out_specs=P("seg", "col"), check_vma=False
    )
```

```python
import functools
import math

import jax
import jax.numpy as jnp
from jax import lax
from jax.experimental import pallas as pl
from jax.experimental.pallas import tpu as pltpu
from jax.sharding import PartitionSpec as P

PANEL = 1024
F32 = jnp.float32
BF16 = jnp.bfloat16
CONTRACT_ROWS = (((0,), (0,)), ((), ()))


def toeplitz(taps_row, width):
    lag = lax.broadcasted_iota(jnp.int32, (width, 2 * width), 0)
    col = lax.broadcasted_iota(jnp.int32, (width, 2 * width), 1)
    flip = (lag + col == width).astype(F32).astype(BF16)
    first = jnp.dot(jnp.broadcast_to(taps_row, (16, width)), flip, preferred_element_type=F32)
    tall = jnp.broadcast_to(first[:1], (width, 2 * width))
    return pltpu.roll(tall, 0, 1, stride=1, stride_axis=0)


def segment_matrix(base, own, joined):
    width = base.shape[0]
    tall = jnp.broadcast_to(own, (width, width)).T
    same = jnp.concatenate([tall, tall], axis=1) == jnp.broadcast_to(joined, (width, 2 * width))
    return jnp.where(same, base, 0.0).astype(BF16)


def cut_pieces(where_ref, rows_ref, pieces, plan):
    for piece, parts in zip(pieces, plan, strict=True):
        at, lanes = 0, piece.shape[1]
        for lo, hi, group in parts:
            start = ((where_ref[0] ^ ORDER[group]) * 2 + where_ref[1]) * lanes
            cols = pl.ds(pl.multiple_of(start, 128), lanes)
            piece[at : at + hi - lo] = rows_ref[lo:hi, cols]
            at += hi - lo


def inner_kernel(where_ref, home_ref, row_ref, taps_ref, sid_ref, design_ref, out_ref, base_ref, owner_ref):
    nblocks, width = sid_ref.shape
    owner_ref[0] = home_ref[row_ref[0]]
    base = toeplitz(taps_ref[...], width)
    base_ref[...] = base.astype(BF16)
    sid = sid_ref[...]
    for b in range(1, nblocks):
        joined = jnp.concatenate([sid[b - 1 : b], sid[b : b + 1]], axis=1)
        matrix = segment_matrix(base, sid[b : b + 1], joined)
        rows = design_ref[(b - 1) * width : (b + 1) * width]
        out_ref[(b - 1) * width : b * width] = jnp.dot(
            matrix, rows, preferred_element_type=F32
        ).astype(BF16)


def rim_kernel(plan, where_ref, base_ref, sid_ref, design_ref, rim_ref, inner_ref, out_ref, *pieces):
    width = sid_ref.shape[1]
    sid = sid_ref[:1]
    rim_sid = rim_ref[width : width + 16, :width].astype(F32)[:1].astype(jnp.int32)
    rim_sid = jnp.where(where_ref[0] + where_ref[1] == 0, -1, rim_sid)
    joined = jnp.concatenate([rim_sid, sid], axis=1)
    matrix = segment_matrix(base_ref[...].astype(F32), sid, joined)
    rows = jnp.concatenate([rim_ref[:width], design_ref[:width]], axis=0)
    out_ref[:width] = jnp.dot(matrix, rows, preferred_element_type=F32).astype(BF16)
    out_ref[width:] = inner_ref[...]
    cut_pieces(where_ref, out_ref, pieces, plan)


VMEM = pl.BlockSpec(memory_space=pltpu.VMEM)
SMEM = pl.BlockSpec(memory_space=pltpu.SMEM)


def piece_shape(rows, plan):
    return [jax.ShapeDtypeStruct((sum(hi - lo for lo, hi, _ in parts), LANES), BF16) for parts in plan]


def last_rows(sid, design, width):
    row = jnp.zeros((16, design.shape[1]), BF16).at[0, :width].set(sid[-width:].astype(BF16))
    return jnp.concatenate([design[-width:], row], axis=0)


def filter_inner(where, home, row, taps, sid, design):
    rows, cols = design.shape
    width = taps.shape[0]
    shapes = [
        jax.ShapeDtypeStruct((rows - width, cols), BF16),
        jax.ShapeDtypeStruct((width, 2 * width), BF16),
        jax.ShapeDtypeStruct((1,), jnp.int32),
    ]
    return pl.pallas_call(
        inner_kernel,
        in_specs=[SMEM] * 3 + [VMEM] * 3,
        out_specs=[VMEM] * 2 + [SMEM],
        out_shape=shapes,
        compiler_params=pltpu.CompilerParams(vmem_limit_bytes=8 << 20),
    )(where, home, row, taps.reshape(1, width), sid.reshape(-1, width), design)


def filter_rim(where, base, sid, design, rim, inner, plan):
    rows, cols = design.shape
    width = base.shape[0]
    shapes = [jax.ShapeDtypeStruct((rows, cols), BF16)] + piece_shape(rows, plan)
    return pl.pallas_call(
        functools.partial(rim_kernel, plan),
        in_specs=[SMEM] + [VMEM] * 5,
        out_specs=[VMEM] * len(shapes),
        out_shape=shapes,
        compiler_params=pltpu.CompilerParams(vmem_limit_bytes=8 << 20),
    )(where, base, sid.reshape(-1, width), design, rim, inner)


def tile(panel, rows):
    return lax.dot_general(panel, rows, CONTRACT_ROWS, preferred_element_type=F32)


def from_before(value):
    nseg = lax.axis_size("seg")
    with jax.named_scope("rim"):
        return lax.ppermute(value, "seg", [(s, (s + 1) % nseg) for s in range(nseg)])


def exchanged(value, bits, name):
    nseg = lax.axis_size("seg")
    with jax.named_scope(f"swap_{name}"):
        return lax.ppermute(value, "seg", [(s, s ^ bits) for s in range(nseg)])


ORDER = (3, 1, 2, 0)
LANES = 128
OUTER = ((2, 0), (3, 1))
INNER = ((2, 0), (3, 1))


def hop(value, pairs, name):
    with jax.named_scope(f"step_{name}"):
        return lax.ppermute(value, "col", pairs)


def sliced_panel(owner, where, rows, *own):
    place = lax.axis_index("col")
    middle = (2, 2, 1, 1)[owner]
    half = rows.shape[0]
    theirs = exchanged(rows, 1, "pair")
    cols = [((where[0] ^ k) * 2 + where[1]) * LANES for k in ORDER]
    other = [lax.dynamic_slice_in_dim(theirs, c, LANES, axis=1) for c in cols]
    pieces = [jnp.concatenate([o, p], axis=0) for o, p in zip(own, other)]
    inside = owner in (1, 2)
    got = [hop(piece, [(owner, middle)], f"a{n}") for n, piece in enumerate(pieces[:2])]
    end = 3 if owner < 2 else 0
    side, source = (3 - end, owner) if inside else (3 - middle, middle)
    sums, landed, far = [None] * 4, [None] * 4, []

    def summed(group, own, paired):
        total = tile(own, rows) + tile(paired, theirs)
        if ORDER[group]:
            sums[group] = total.astype(BF16)
            landed[group] = exchanged(sums[group], 2 * ORDER[group], f"g{group}")
        return total

    for n, piece in enumerate(pieces):
        held = got[n]
        for at, group in INNER if inside else OUTER:
            if at == n:
                held, sums[group] = lax.optimization_barrier((held, sums[group]))
        if n < 2:
            both = jnp.where(place == owner, pieces[n + 2], held)
            got.append(hop(both, [(owner, middle), (middle, end)], f"m{n}"))
            out = got[-1]
        elif inside:
            both = jnp.where(place == owner, piece, held)
            out = hop(both, [(owner, side), (middle, end)], f"b{n}")
        else:
            out = hop(held, [(middle, end)], f"c{n}")
        if n < 2 or not inside:
            given = hop(piece if inside else held, [(source, side)], f"b{n}")
            out = jnp.where(place == side, given, out)
        far.append(jnp.where(place == owner, piece, jnp.where(place == middle, held, out)))
        panel = far[n]
        total = summed(n, panel[:half], panel[half:])
    for part in landed[:3]:
        total = total + part.astype(F32)
    return total


def spread(value, axis, source):
    kept = jnp.where(lax.axis_index(axis) == source, value, 0).astype(value.dtype)
    return lax.psum(kept, axis)


def any_mesh(owner, where, rows):
    panel = spread(rows, "col", owner)
    return lax.psum_scatter(tile(panel, rows), "seg", scatter_dimension=0, tiled=True)


def solution(mesh):
    nseg, ncol = mesh.shape["seg"], mesh.shape["col"]

    def shards(design, taps, seg_ids, block_home, block_row):
        sliced = (nseg, ncol, design.shape[1]) == (8, 4, PANEL)
        scale = 1.0 / math.sqrt(design.shape[0] * nseg)
        seg = lax.axis_index("seg")
        where = jnp.stack([lax.shift_right_logical(seg, 1), seg & 1]).astype(jnp.int32)
        rim = from_before(last_rows(seg_ids, design, taps.shape[0]))
        inner, base, home = filter_inner(where, block_home, block_row, taps, seg_ids, design)
        owner = home[0] // (design.shape[1] // PANEL)
        count = design.shape[0]
        plan = [((0, count, n),) for n in range(len(ORDER))]
        made = filter_rim(where, base, seg_ids, design, rim, inner, plan if sliced else [])
        if sliced:
            branches = [lambda *a, o=o: sliced_panel(o, *a) * scale for o in range(ncol)]
            return lax.switch(owner, branches, where, *made)
        return any_mesh(owner, where, *made) * scale

    placed = (P("seg", "col"), P(), P("seg"), P(), P())
    return jax.shard_map(
        shards, mesh=mesh, in_specs=placed, out_specs=P("seg", "col"), check_vma=False
    )
```

```python
import functools
import math

import jax
import jax.numpy as jnp
from jax import lax
from jax.experimental import pallas as pl
from jax.experimental.pallas import tpu as pltpu
from jax.sharding import PartitionSpec as P

PANEL = 1024
F32 = jnp.float32
BF16 = jnp.bfloat16
CONTRACT_ROWS = (((0,), (0,)), ((), ()))


def toeplitz(taps_row, width):
    lag = lax.broadcasted_iota(jnp.int32, (width, 2 * width), 0)
    col = lax.broadcasted_iota(jnp.int32, (width, 2 * width), 1)
    flip = (lag + col == width).astype(F32).astype(BF16)
    first = jnp.dot(jnp.broadcast_to(taps_row, (16, width)), flip, preferred_element_type=F32)
    tall = jnp.broadcast_to(first[:1], (width, 2 * width))
    return pltpu.roll(tall, 0, 1, stride=1, stride_axis=0)


def segment_matrix(base, own, joined):
    width = base.shape[0]
    tall = jnp.broadcast_to(own, (width, width)).T
    same = jnp.concatenate([tall, tall], axis=1) == jnp.broadcast_to(joined, (width, 2 * width))
    return jnp.where(same, base, 0.0).astype(BF16)


def cut_pieces(where_ref, rows_ref, pieces, plan):
    for piece, parts in zip(pieces, plan, strict=True):
        at, lanes = 0, piece.shape[1]
        for lo, hi, group, flip in parts:
            start = ((where_ref[0] ^ ORDER[group]) * 2 + (where_ref[1] ^ flip)) * lanes
            cols = pl.ds(pl.multiple_of(start, 128), lanes)
            piece[at : at + hi - lo] = rows_ref[lo:hi, cols]
            at += hi - lo


def inner_kernel(where_ref, home_ref, row_ref, taps_ref, sid_ref, design_ref, out_ref, base_ref, owner_ref):
    nblocks, width = sid_ref.shape
    owner_ref[0] = home_ref[row_ref[0]]
    base = toeplitz(taps_ref[...], width)
    base_ref[...] = base.astype(BF16)
    sid = sid_ref[...]
    for b in range(1, nblocks):
        joined = jnp.concatenate([sid[b - 1 : b], sid[b : b + 1]], axis=1)
        matrix = segment_matrix(base, sid[b : b + 1], joined)
        rows = design_ref[(b - 1) * width : (b + 1) * width]
        out_ref[(b - 1) * width : b * width] = jnp.dot(
            matrix, rows, preferred_element_type=F32
        ).astype(BF16)


def rim_kernel(plan, where_ref, base_ref, sid_ref, design_ref, rim_ref, inner_ref, out_ref, *pieces):
    width = sid_ref.shape[1]
    sid = sid_ref[:1]
    rim_sid = rim_ref[width : width + 16, :width].astype(F32)[:1].astype(jnp.int32)
    rim_sid = jnp.where(where_ref[0] + where_ref[1] == 0, -1, rim_sid)
    joined = jnp.concatenate([rim_sid, sid], axis=1)
    matrix = segment_matrix(base_ref[...].astype(F32), sid, joined)
    rows = jnp.concatenate([rim_ref[:width], design_ref[:width]], axis=0)
    out_ref[:width] = jnp.dot(matrix, rows, preferred_element_type=F32).astype(BF16)
    out_ref[width:] = inner_ref[...]
    cut_pieces(where_ref, out_ref, pieces, plan)


VMEM = pl.BlockSpec(memory_space=pltpu.VMEM)
SMEM = pl.BlockSpec(memory_space=pltpu.SMEM)


def piece_shape(rows, plan):
    return [jax.ShapeDtypeStruct((sum(hi - lo for lo, hi, *_ in parts), LANES), BF16) for parts in plan]


def last_rows(sid, design, width):
    row = jnp.zeros((16, design.shape[1]), BF16).at[0, :width].set(sid[-width:].astype(BF16))
    return jnp.concatenate([design[-width:], row], axis=0)


def filter_inner(where, home, row, taps, sid, design):
    rows, cols = design.shape
    width = taps.shape[0]
    shapes = [
        jax.ShapeDtypeStruct((rows - width, cols), BF16),
        jax.ShapeDtypeStruct((width, 2 * width), BF16),
        jax.ShapeDtypeStruct((1,), jnp.int32),
    ]
    return pl.pallas_call(
        inner_kernel,
        in_specs=[SMEM] * 3 + [VMEM] * 3,
        out_specs=[VMEM] * 2 + [SMEM],
        out_shape=shapes,
        compiler_params=pltpu.CompilerParams(vmem_limit_bytes=8 << 20),
    )(where, home, row, taps.reshape(1, width), sid.reshape(-1, width), design)


def filter_rim(where, base, sid, design, rim, inner, plan):
    rows, cols = design.shape
    width = base.shape[0]
    shapes = [jax.ShapeDtypeStruct((rows, cols), BF16)] + piece_shape(rows, plan)
    return pl.pallas_call(
        functools.partial(rim_kernel, plan),
        in_specs=[SMEM] + [VMEM] * 5,
        out_specs=[VMEM] * len(shapes),
        out_shape=shapes,
        compiler_params=pltpu.CompilerParams(vmem_limit_bytes=8 << 20),
    )(where, base, sid.reshape(-1, width), design, rim, inner)


def stack_kernel(other_ref, *refs):
    half = len(refs) // 2
    for n, (own, piece) in enumerate(zip(refs[:half], refs[half:])):
        rows = own.shape[0]
        piece[:rows] = own[...]
        piece[rows:] = other_ref[n * rows : (n + 1) * rows]


def stacked(other, own):
    rows, lanes = own[0].shape
    return pl.pallas_call(
        stack_kernel,
        in_specs=[VMEM] * (len(own) + 1),
        out_specs=[VMEM] * len(own),
        out_shape=[jax.ShapeDtypeStruct((2 * rows, lanes), BF16)] * len(own),
        compiler_params=pltpu.CompilerParams(vmem_limit_bytes=8 << 20),
    )(other, *own)


def tile(panel, rows):
    return lax.dot_general(panel, rows, CONTRACT_ROWS, preferred_element_type=F32)


def from_before(value):
    nseg = lax.axis_size("seg")
    with jax.named_scope("rim"):
        return lax.ppermute(value, "seg", [(s, (s + 1) % nseg) for s in range(nseg)])


def exchanged(value, bits, name):
    nseg = lax.axis_size("seg")
    with jax.named_scope(f"swap_{name}"):
        return lax.ppermute(value, "seg", [(s, s ^ bits) for s in range(nseg)])


ORDER = (3, 1, 2, 0)
LANES = 128
OUTER = ((2, 0), (3, 1))
INNER = ((2, 0), (3, 1))


def hop(value, pairs, name):
    with jax.named_scope(f"step_{name}"):
        return lax.ppermute(value, "col", pairs)


def sliced_panel(owner, rows, given, *own):
    place = lax.axis_index("col")
    middle = (2, 2, 1, 1)[owner]
    half = rows.shape[0]
    theirs = exchanged(rows, 1, "pair")
    other = exchanged(given, 1, "given")
    pieces = stacked(other, own)
    inside = owner in (1, 2)
    got = [hop(piece, [(owner, middle)], f"a{n}") for n, piece in enumerate(pieces[:2])]
    end = 3 if owner < 2 else 0
    side, source = (3 - end, owner) if inside else (3 - middle, middle)
    sums, landed, far = [None] * 4, [None] * 4, []

    def summed(group, own, paired):
        total = tile(own, rows) + tile(paired, theirs)
        if ORDER[group]:
            sums[group] = total.astype(BF16)
            landed[group] = exchanged(sums[group], 2 * ORDER[group], f"g{group}")
        return total

    for n, piece in enumerate(pieces):
        held = got[n]
        for at, group in INNER if inside else OUTER:
            if at == n:
                held, sums[group] = lax.optimization_barrier((held, sums[group]))
        if n < 2:
            both = jnp.where(place == owner, pieces[n + 2], held)
            got.append(hop(both, [(owner, middle), (middle, end)], f"m{n}"))
            out = got[-1]
        elif inside:
            both = jnp.where(place == owner, piece, held)
            out = hop(both, [(owner, side), (middle, end)], f"b{n}")
        else:
            out = hop(held, [(middle, end)], f"c{n}")
        if n < 2 or not inside:
            given = hop(piece if inside else held, [(source, side)], f"b{n}")
            out = jnp.where(place == side, given, out)
        far.append(jnp.where(place == owner, piece, jnp.where(place == middle, held, out)))
        panel = far[n]
        total = summed(n, panel[:half], panel[half:])
    for part in landed[:3]:
        total = total + part.astype(F32)
    return total


def spread(value, axis, source):
    kept = jnp.where(lax.axis_index(axis) == source, value, 0).astype(value.dtype)
    return lax.psum(kept, axis)


def any_mesh(owner, rows):
    panel = spread(rows, "col", owner)
    return lax.psum_scatter(tile(panel, rows), "seg", scatter_dimension=0, tiled=True)


def solution(mesh):
    nseg, ncol = mesh.shape["seg"], mesh.shape["col"]

    def shards(design, taps, seg_ids, block_home, block_row):
        sliced = (nseg, ncol, design.shape[1]) == (8, 4, PANEL)
        scale = 1.0 / math.sqrt(design.shape[0] * nseg)
        seg = lax.axis_index("seg")
        where = jnp.stack([lax.shift_right_logical(seg, 1), seg & 1]).astype(jnp.int32)
        rim = from_before(last_rows(seg_ids, design, taps.shape[0]))
        inner, base, home = filter_inner(where, block_home, block_row, taps, seg_ids, design)
        owner = home[0] // (design.shape[1] // PANEL)
        count = design.shape[0]
        groups = range(len(ORDER))
        plan = [tuple((0, count, n, 1) for n in groups)] + [((0, count, n, 0),) for n in groups]
        made = filter_rim(where, base, seg_ids, design, rim, inner, plan if sliced else [])
        if sliced:
            branches = [lambda *a, o=o: sliced_panel(o, *a) * scale for o in range(ncol)]
            return lax.switch(owner, branches, *made)
        return any_mesh(owner, *made) * scale

    placed = (P("seg", "col"), P(), P("seg"), P(), P())
    return jax.shard_map(
        shards, mesh=mesh, in_specs=placed, out_specs=P("seg", "col"), check_vma=False
    )
```
